32 devices in a mesh: grp: 2 (over x), tile: 16 (over z, y, core).
Axes of the slice: x: 2, y: 2, z: 4, core: 2. Of those that a mesh axis runs over, the one named last changes fastest.
Arguments:
- site_cell: int32 [2048, 2], P(('grp', 'tile')), may hold values from 0 to 63
- site_power: float32 [2048], P(('grp', 'tile')), may hold values from -4.5 to -2
- site_tile: int32 [2048, 1], P(('grp', 'tile')), may hold values from 0 to 15; in each aligned block of 64 rows (0 to 63, 64 to 127, ...) at most 8 rows name the same one
- shadow: bfloat16 [2048, 4096], P(('grp', 'tile')), may hold values from -3.75 to 3.75
Outputs:
- count_dist: float32 [16, 8, 4096], P('tile', None, 'grp')
The draws below stay inside these ranges and needn't reach their ends.
Inputs may be any that keep to these rules, and one draw needn't show every extreme that they name: `site_tile`: among the 64 sites of one device (aligned blocks of rows), at most 8 name the same tile; in some devices a tile is named by exactly 8.
All inputs are finite; a program needn't handle non-finite values.
Results may differ from the reference program's by a relative error of at most 0.00075.
Values may be sent and summed in bfloat16 or wider, within the bound.
No kernel may reach another device: no remote copies, remote signals or barrier semaphores. Data moves between devices by JAX's collectives and lax.ppermute only.
A program may use at most 64 MiB of HBM per device.

```python
import math
import jax
import jax.numpy as jnp
import numpy as np
from jax import lax

WIN = 64
KMAX = 8
SITE_DEV = 64
CAP = 8
SITES = 2048
TILES = 16
CELLS = 4096
N_TILE = 16


def touch_ends(array, rng, least, top_value):
    spot = [jax.random.randint(jax.random.fold_in(rng, axis), (), 0, length) for axis, length in enumerate(array.shape)]
    widest = array.shape.index(max(array.shape))
    neighbour = spot[:widest] + [(spot[widest] + 1) % array.shape[widest]] + spot[widest + 1:]
    return array.at[tuple(spot)].set(least).at[tuple(neighbour)].set(top_value)


def block_scale(stream_key, shape, cuts, smallest, high):
    def one(dim, blocks):
        heights = jax.random.uniform(jax.random.fold_in(jax.random.fold_in(stream_key, 6), dim), (blocks,), jnp.float32, smallest / len(cuts), high / len(cuts))
        return jnp.repeat(jnp.exp(heights), shape[dim] // blocks).reshape((-1,) + (1,) * (len(shape) - dim - 1))

    gain = one(*cuts[0])
    for cut in cuts[1:]:
        gain = gain * one(*cut)
    return gain


def routed_block(stream_key, own, number, rows, number_of, top, limit, lean):
    sequence = jax.random.permutation(stream_key, number_of)
    heavy_load, ordinary = portions_of(number_of, rows * top, limit, lean, True), portions_of(number_of, rows * top, limit, lean, False)
    places = jnp.arange(number_of)

    def named(sizes, turn):
        used = int((sizes > 0).sum())
        fixed = max(1, used // 4)
        passed = fixed + (places - fixed + turn * (used - fixed)) % max(1, number_of - fixed)
        return jnp.zeros((number_of,), jnp.int32).at[sequence[jnp.where(places < fixed, places, passed)]].set(jnp.asarray(sizes, jnp.int32))

    sizes = jnp.where(number % 4 == 0, named(heavy_load, number // 4), named(ordinary, number - number // 4 - 1))
    mixed = jax.random.permutation(jax.random.fold_in(own, 3), number_of)
    source_of, taker = mixed[0:number_of // 2 * 2:2], mixed[1:number_of // 2 * 2:2]
    room = jnp.minimum(sizes[source_of] - 1, limit - sizes[taker]) // 2
    room = jnp.where((source_of == sequence[0]) | (taker == sequence[0]) | (sizes[taker] == 0), 0, jnp.maximum(room, 0))
    passed = jax.random.randint(jax.random.fold_in(own, 4), (number_of // 2,), 0, 1 << 20) % (room + 1)
    sizes = sizes.at[source_of].add(-passed).at[taker].add(passed)
    members = jnp.searchsorted(jnp.cumsum(sizes), jnp.arange(rows * top), side="right").astype(jnp.int32)
    listing = members.reshape(top, rows).T
    listing = listing[jax.random.permutation(jax.random.fold_in(own, 1), rows)]
    turn = jax.random.randint(jax.random.fold_in(own, 2), (rows, 1), 0, top)
    return jnp.take_along_axis(listing, (jnp.arange(top)[None, :] + turn) % top, axis=1)


def portions_of(amount, total, limit, lean, full):
    loads = [(1 << 20) // math.isqrt(grade ** lean) + 1 for grade in range(1, amount + 1)]
    largest = limit if full else min(limit, max(-(-total // amount), total * loads[0] // sum(loads)))
    least = 1 if total - largest >= amount - 1 else 0
    given, surplus = [largest] + [least] * (amount - 1), total - largest - least * (amount - 1)
    while surplus > 0:
        movable = [i for i in range(1, amount) if given[i] < largest] or [i for i in range(1, amount) if given[i] < limit]
        mass, remaining = sum([loads[i] for i in movable]), surplus
        for i in movable:
            addition = min(limit - given[i], max(1, remaining * loads[i] // mass), surplus)
            given[i] = given[i] + addition
            surplus = surplus - addition
    return np.array(given)


def scatter_about(own_key, shape, deviation, reach, split=(), kind=jnp.bfloat16):
    entries = deviation * jax.random.normal(own_key, shape, jnp.float32)
    if split:
        entries = entries * block_scale(own_key, shape, split, -0.22, 0.18)
    return jnp.clip(entries, -reach, reach).astype(kind)


def setup_inputs(seed: int = 0) -> dict:
    arg_keys = jax.random.split(jax.random.key(seed), 5)
    site_cell = touch_ends(jax.random.randint(arg_keys[0], (SITES, 2), 0, WIN), jax.random.fold_in(arg_keys[0], 1), 0, WIN - 1).astype(jnp.int32)
    site_power = jnp.clip(-4.5 + 2.5 * jax.random.uniform(arg_keys[1], (SITES,), jnp.float32) ** block_scale(arg_keys[1], (SITES,), ((0, 32),), -0.2, 0.2), -4.5, -2.0)
    site_tile_keys = jax.random.split(jax.random.fold_in(arg_keys[2], 1), SITES // SITE_DEV)
    site_tile_turns = jax.random.permutation(jax.random.fold_in(arg_keys[2], 3), SITES // SITE_DEV)
    site_tile = jax.vmap(lambda own, number: routed_block(jax.random.fold_in(arg_keys[2], 2), own, number, SITE_DEV, N_TILE, 1, CAP, 2))(site_tile_keys, site_tile_turns).reshape((SITES, 1))
    shadow = scatter_about(arg_keys[3], (SITES, CELLS), 1.5, 3.75, ((0, 32),))
    return {"site_cell": site_cell, "site_power": site_power, "site_tile": site_tile, "shadow": shadow}


reach_sq = 16.0


def reference(site_cell, site_power, site_tile, shadow):
    cell_index = jnp.arange(CELLS, dtype=jnp.int32)
    cell_row = (cell_index // WIN).astype(jnp.float32)
    cell_col = (cell_index % WIN).astype(jnp.float32)
    initial = jnp.zeros((TILES, KMAX, CELLS), jnp.float32).at[:, 0, :].set(1.0)

    def add_site(state_table, site_data):
        position, tx_power, tile_slot, window = site_data
        row_gap = cell_row - position[0].astype(jnp.float32)
        col_gap = cell_col - position[1].astype(jnp.float32)
        margin = tx_power - jnp.log(1.0 + (row_gap * row_gap + col_gap * col_gap) / reach_sq) + window.astype(jnp.float32)
        rounded = jax.nn.sigmoid(margin).astype(jnp.bfloat16)
        detect_prob = lax.optimization_barrier(rounded).astype(jnp.float32)
        previous = lax.dynamic_index_in_dim(state_table, tile_slot, 0, keepdims=False)
        shifted = jnp.concatenate([jnp.zeros((1, CELLS), jnp.float32), previous[:-1]], axis=0)
        updated = previous * (1.0 - detect_prob) + shifted * detect_prob
        state_table = lax.dynamic_update_index_in_dim(state_table, updated, tile_slot, 0)
        return state_table, None

    state_table, unused = lax.scan(add_site, initial, (site_cell, site_power, site_tile[:, 0].astype(jnp.int32), shadow))
    return state_table
```

```python
import functools

import jax
import jax.numpy as jnp
from jax import lax
from jax.experimental import pallas as pl
from jax.experimental.pallas import tpu as pltpu
from jax.sharding import Mesh, PartitionSpec as P

WIN = 64
KMAX = 8
LANES = 128

reach_sq = 16.0


def column(row_values):
    n = row_values.shape[1]
    on_diagonal = lax.broadcasted_iota(jnp.int32, (n, n), 0) == lax.broadcasted_iota(
        jnp.int32, (n, n), 1
    )
    return jnp.sum(jnp.where(on_diagonal, row_values, 0.0), axis=1, keepdims=True)


def probs_kernel(tiles, cell_ref, power_ref, tile_ref, shadow_ref, out_ref):
    sites = shadow_ref.shape[0]
    receivers = out_ref.shape[0]
    strips = shadow_ref.shape[1] // receivers // LANES
    tile_row = tile_ref[...].astype(jnp.float32)
    before = lax.broadcasted_iota(jnp.int32, (sites, sites), 0) < lax.broadcasted_iota(
        jnp.int32, (sites, sites), 1
    )
    same = column(tile_row) == tile_row
    rank = jnp.sum(jnp.where(same & before, 1.0, 0.0), axis=0, keepdims=True)
    slot = rank * tiles + tile_row
    slot_rows = jnp.broadcast_to(
        jnp.concatenate([slot] * (LANES // sites), axis=1), (8, LANES)
    ).astype(jnp.bfloat16)

    lane = lax.broadcasted_iota(jnp.int32, (sites, LANES), 1)
    cell = cell_ref[...].astype(jnp.float32)
    row_gap = (lane // WIN).astype(jnp.float32) - column(cell[0:1, :])
    col_gap = (lane % WIN).astype(jnp.float32) - column(cell[1:2, :])
    col_part = 1.0 + col_gap * col_gap / reach_sq
    row_quarter = row_gap * 0.25
    power = jnp.broadcast_to(column(power_ref[...]), (sites, LANES))

    for block in range(receivers):
        for strip in range(strips):
            first = (block * strips + strip) * LANES
            window = shadow_ref[:, first : first + LANES].astype(jnp.float32)
            row_part = row_quarter + (first // WIN) * 0.25
            loss = col_part + row_part * row_part
            odds_against = loss * jnp.exp(-(power + window))
            out_ref[block, strip * sites : (strip + 1) * sites, :] = (
                1.0 / (1.0 + odds_against)
            ).astype(jnp.bfloat16)
        out_ref[block, strips * sites : strips * sites + 8, :] = slot_rows


def count_kernel(tiles, capacity, sites, blocks_ref, out_ref, even_ref, odd_ref):
    senders = blocks_ref.shape[0]
    strips = even_ref.shape[1] // LANES
    slots = tiles * capacity
    slot_number = lax.broadcasted_iota(jnp.int32, (slots, sites), 0).astype(jnp.float32)

    def place(sender, slots_ref):
        named = blocks_ref[sender, pl.ds(strips * sites, 8), :].astype(jnp.float32)
        selector = (slot_number == named[0:1, :sites]).astype(jnp.bfloat16)
        for strip in range(strips):
            probs = blocks_ref[sender, strip * sites : (strip + 1) * sites, :]
            slots_ref[:, strip * LANES : (strip + 1) * LANES] = jnp.dot(
                selector, probs, preferred_element_type=jnp.float32
            )

    def add_pair(states, hit_a, hit_b):
        miss_a = 1.0 - hit_a
        miss_b = 1.0 - hit_b
        none = miss_a * miss_b
        both = hit_a * hit_b
        one = (hit_a + hit_b) - (both + both)
        new = []
        for k in range(KMAX):
            term = states[k] * none
            if k >= 1:
                term = term + states[k - 1] * one
            if k >= 2:
                term = term + states[k - 2] * both
            new.append(term)
        return new

    def add_sender(states, slots_ref):
        for rank in range(0, capacity, 2):
            states = add_pair(
                states,
                slots_ref[rank * tiles : (rank + 1) * tiles, :],
                slots_ref[(rank + 1) * tiles : (rank + 2) * tiles, :],
            )
        return states

    width = even_ref.shape[1]
    states = [jnp.ones((tiles, width), jnp.float32)] + [
        jnp.zeros((tiles, width), jnp.float32) for _ in range(KMAX - 1)
    ]
    place(0, even_ref)

    def step(i, states):
        place(2 * i + 1, odd_ref)
        states = add_sender(list(states), even_ref)
        place(jnp.minimum(2 * i + 2, senders - 1), even_ref)
        return tuple(add_sender(states, odd_ref))

    states = lax.fori_loop(0, senders // 2, step, tuple(states))
    for k in range(KMAX):
        for strip in range(strips):
            out_ref[pl.ds(strip * KMAX + k, tiles, stride=strips * KMAX), :] = states[k][
                :, strip * LANES : (strip + 1) * LANES
            ]


def merge_kernel(parts, in_ref, out_ref):
    pieces = in_ref.shape[0] // parts
    strips = in_ref.shape[1] // KMAX
    count = lax.broadcasted_iota(jnp.int32, (KMAX, LANES), 0)
    for piece in range(pieces):
        for strip in range(strips):
            rows = slice(strip * KMAX, (strip + 1) * KMAX)
            total = in_ref[piece, rows, :]
            for part in range(1, parts):
                other = in_ref[part * pieces + piece, rows, :]
                joint = other * total[0:1, :]
                for k in range(1, KMAX):
                    shifted = jnp.where(count >= k, pltpu.roll(other, k, 0), 0.0)
                    joint = joint + shifted * total[k : k + 1, :]
                total = joint
            first = (piece * strips + strip) * LANES
            out_ref[0, :, first : first + LANES] = total


def on_device(site_cell, site_power, site_tile, shadow):
    groups = lax.axis_size("grp")
    parts = lax.axis_size("far")
    near = lax.axis_size("near")
    tiles = parts * near
    sites, cells = shadow.shape
    capacity = max(2, 2 * sites // tiles)
    receivers = groups * near
    width = cells // receivers
    rows = sites * (width // LANES) + 8

    blocks = pl.pallas_call(
        functools.partial(probs_kernel, tiles),
        out_shape=jax.ShapeDtypeStruct((receivers, rows, LANES), jnp.bfloat16),
        name="probs",
    )(site_cell.T, site_power[None, :], site_tile.T, shadow)
    blocks = lax.all_to_all(blocks, ("grp", "near"), split_axis=0, concat_axis=0, tiled=True)
    dist = pl.pallas_call(
        functools.partial(count_kernel, tiles, capacity, sites),
        out_shape=jax.ShapeDtypeStruct((tiles * KMAX * width // LANES, LANES), jnp.float32),
        scratch_shapes=[pltpu.VMEM((tiles * capacity, width), jnp.float32)] * 2,
        name="counts",
    )(blocks)
    dist = dist.reshape(tiles, KMAX * width // LANES, LANES)
    dist = lax.all_to_all(dist, ("far", "near"), split_axis=0, concat_axis=0, tiled=True)
    return pl.pallas_call(
        functools.partial(merge_kernel, parts),
        out_shape=jax.ShapeDtypeStruct((1, KMAX, cells // groups), jnp.float32),
        name="merge",
    )(dist)


def solution(mesh):
    groups, tiles = mesh.shape["grp"], mesh.shape["tile"]
    near = min(tiles // 2, max(1, WIN * WIN // LANES // groups))
    split = Mesh(mesh.devices.reshape(groups, tiles // near, near), ("grp", "far", "near"))
    everywhere = ("grp", "far", "near")
    placed = (P(everywhere, None), P(everywhere), P(everywhere, None), P(everywhere, None))
    return jax.shard_map(
        on_device,
        mesh=split,
        in_specs=placed,
        out_specs=P(("far", "near"), None, "grp"),
        check_vma=False,
    )
```

```python
import functools

import jax
import jax.numpy as jnp
from jax import lax
from jax.experimental import pallas as pl
from jax.experimental.pallas import tpu as pltpu
from jax.sharding import Mesh, PartitionSpec as P

WIN = 64
KMAX = 8
LANES = 128

reach_sq = 16.0


def column(row_values):
    n = row_values.shape[1]
    on_diagonal = lax.broadcasted_iota(jnp.int32, (n, n), 0) == lax.broadcasted_iota(
        jnp.int32, (n, n), 1
    )
    return jnp.sum(jnp.where(on_diagonal, row_values, 0.0), axis=1, keepdims=True)


def probs_kernel(
    tiles, cell_hbm, power_hbm, tile_hbm, shadow_hbm, out_ref, cell_ref, power_ref, tile_ref, shadow_ref, sems
):
    sites = shadow_ref.shape[0]
    receivers = out_ref.shape[0]
    strips = shadow_ref.shape[1] // receivers // LANES
    pieces = sems.shape[0] - 3
    span = shadow_ref.shape[1] // pieces
    small = [
        pltpu.make_async_copy(source, target, sems.at[pieces + i])
        for i, (source, target) in enumerate(
            [(cell_hbm, cell_ref), (power_hbm, power_ref), (tile_hbm, tile_ref)]
        )
    ]
    windows = []
    for i in range(pieces):
        part = slice(i * span, (i + 1) * span)
        windows.append(
            pltpu.make_async_copy(shadow_hbm.at[:, part], shadow_ref.at[:, part], sems.at[i])
        )
    for copy in small + windows:
        copy.start()
    for copy in small:
        copy.wait()
    tile_row = tile_ref[...].astype(jnp.float32)
    before = lax.broadcasted_iota(jnp.int32, (sites, sites), 0) < lax.broadcasted_iota(
        jnp.int32, (sites, sites), 1
    )
    same = column(tile_row) == tile_row
    rank = jnp.sum(jnp.where(same & before, 1.0, 0.0), axis=0, keepdims=True)
    slot = rank * tiles + tile_row
    slot_rows = jnp.broadcast_to(
        jnp.concatenate([slot] * (LANES // sites), axis=1), (8, LANES)
    ).astype(jnp.bfloat16)

    lane = lax.broadcasted_iota(jnp.int32, (sites, LANES), 1)
    cell = cell_ref[...].astype(jnp.float32)
    row_gap = (lane // WIN).astype(jnp.float32) - column(cell[0:1, :])
    col_gap = (lane % WIN).astype(jnp.float32) - column(cell[1:2, :])
    col_part = 1.0 + col_gap * col_gap / reach_sq
    row_quarter = row_gap * 0.25
    power = jnp.broadcast_to(column(power_ref[...]), (sites, LANES))

    for block in range(receivers):
        out_ref[block, strips * sites : strips * sites + 8, :] = slot_rows
        for strip in range(strips):
            first = (block * strips + strip) * LANES
            if first % span == 0:
                windows[first // span].wait()
            window = shadow_ref[:, first : first + LANES].astype(jnp.float32)
            row_part = row_quarter + (first // WIN) * 0.25
            loss = col_part + row_part * row_part
            odds_against = loss * jnp.exp(-(power + window))
            out_ref[block, strip * sites : (strip + 1) * sites, :] = (
                1.0 / (1.0 + odds_against)
            ).astype(jnp.bfloat16)


def count_kernel(tiles, capacity, sites, blocks_ref, out_ref, even_ref, odd_ref):
    senders = blocks_ref.shape[0]
    strips = even_ref.shape[1] // LANES
    slots = tiles * capacity
    slot_number = lax.broadcasted_iota(jnp.int32, (slots, sites), 0).astype(jnp.float32)

    def place(sender, slots_ref):
        named = blocks_ref[sender, pl.ds(strips * sites, 8), :].astype(jnp.float32)
        selector = (slot_number == named[0:1, :sites]).astype(jnp.bfloat16)
        probs = jnp.concatenate(
            [blocks_ref[sender, i * sites : (i + 1) * sites, :] for i in range(strips)], axis=1
        )
        slots_ref[...] = jnp.dot(selector, probs, preferred_element_type=jnp.float32)

    def add_pair(states, hit_a, hit_b):
        miss_a = 1.0 - hit_a
        miss_b = 1.0 - hit_b
        none = miss_a * miss_b
        both = hit_a * hit_b
        one = (hit_a + hit_b) - (both + both)
        new = []
        for k in range(KMAX):
            term = states[k] * none
            if k >= 1:
                term = term + states[k - 1] * one
            if k >= 2:
                term = term + states[k - 2] * both
            new.append(term)
        return new

    def add_sender(states, slots_ref):
        for rank in range(0, capacity, 2):
            states = add_pair(
                states,
                slots_ref[rank * tiles : (rank + 1) * tiles, :],
                slots_ref[(rank + 1) * tiles : (rank + 2) * tiles, :],
            )
        return states

    width = even_ref.shape[1]
    states = [jnp.ones((tiles, width), jnp.float32)] + [
        jnp.zeros((tiles, width), jnp.float32) for _ in range(KMAX - 1)
    ]
    refs = [even_ref, odd_ref]
    place(0, refs[0])
    for i in range(senders):
        if i + 1 < senders:
            place(i + 1, refs[(i + 1) % 2])
        states = add_sender(states, refs[i % 2])
    for k in range(KMAX):
        for strip in range(strips):
            out_ref[pl.ds(strip * KMAX + k, tiles, stride=strips * KMAX), :] = states[k][
                :, strip * LANES : (strip + 1) * LANES
            ]


def merge_kernel(parts, in_ref, out_ref):
    pieces = in_ref.shape[0] // parts
    strips = in_ref.shape[1] // KMAX
    count = lax.broadcasted_iota(jnp.int32, (KMAX, LANES), 0)
    for piece in range(pieces):
        for strip in range(strips):
            rows = slice(strip * KMAX, (strip + 1) * KMAX)
            total = in_ref[piece, rows, :]
            for part in range(1, parts):
                other = in_ref[part * pieces + piece, rows, :]
                joint = other * total[0:1, :]
                for k in range(1, KMAX):
                    shifted = jnp.where(count >= k, pltpu.roll(other, k, 0), 0.0)
                    joint = joint + shifted * total[k : k + 1, :]
                total = joint
            first = (piece * strips + strip) * LANES
            out_ref[0, :, first : first + LANES] = total


def on_device(site_cell, site_power, site_tile, shadow):
    groups = lax.axis_size("grp")
    parts = lax.axis_size("far")
    near = lax.axis_size("near")
    tiles = parts * near
    sites, cells = shadow.shape
    capacity = max(2, 2 * sites // tiles)
    receivers = groups * near
    width = cells // receivers
    rows = sites * (width // LANES) + 8

    small = pltpu.CompilerParams(vmem_limit_bytes=8 * 1024 * 1024)
    blocks = pl.pallas_call(
        functools.partial(probs_kernel, tiles),
        out_shape=jax.ShapeDtypeStruct((receivers, rows, LANES), jnp.bfloat16),
        in_specs=[pl.BlockSpec(memory_space=pltpu.HBM)] * 4,
        scratch_shapes=[
            pltpu.VMEM((2, sites), jnp.int32),
            pltpu.VMEM((1, sites), jnp.float32),
            pltpu.VMEM((1, sites), jnp.int32),
            pltpu.VMEM((sites, cells), jnp.bfloat16),
            pltpu.SemaphoreType.DMA((4 + 3,)),
        ],
        compiler_params=small,
        name="probs",
    )(*[
        pltpu.with_memory_space_constraint(x, pltpu.HBM)
        for x in (site_cell.T, site_power[None, :], site_tile.T, shadow)
    ])
    blocks = lax.all_to_all(blocks, ("grp", "near"), split_axis=0, concat_axis=0, tiled=True)
    dist = pl.pallas_call(
        functools.partial(count_kernel, tiles, capacity, sites),
        out_shape=jax.ShapeDtypeStruct((tiles * KMAX * width // LANES, LANES), jnp.float32),
        scratch_shapes=[pltpu.VMEM((tiles * capacity, width), jnp.float32)] * 2,
        compiler_params=small,
        name="counts",
    )(blocks)
    dist = dist.reshape(tiles, KMAX * width // LANES, LANES)
    dist = lax.all_to_all(dist, ("far", "near"), split_axis=0, concat_axis=0, tiled=True)
    return pl.pallas_call(
        functools.partial(merge_kernel, parts),
        out_shape=jax.ShapeDtypeStruct((1, KMAX, cells // groups), jnp.float32),
        compiler_params=small,
        name="merge",
    )(dist)


def solution(mesh):
    groups, tiles = mesh.shape["grp"], mesh.shape["tile"]
    near = min(tiles // 2, max(1, WIN * WIN // LANES // groups))
    split = Mesh(mesh.devices.reshape(groups, tiles // near, near), ("grp", "far", "near"))
    everywhere = ("grp", "far", "near")
    placed = (P(everywhere, None), P(everywhere), P(everywhere, None), P(everywhere, None))
    return jax.shard_map(
        on_device,
        mesh=split,
        in_specs=placed,
        out_specs=P(("far", "near"), None, "grp"),
        check_vma=False,
    )
```

```python
import functools

import jax
import jax.numpy as jnp
from jax import lax
from jax.experimental import pallas as pl
from jax.experimental.pallas import tpu as pltpu
from jax.sharding import Mesh, PartitionSpec as P

WIN = 64
KMAX = 8
LANES = 128

reach_sq = 16.0


def column(row_values):
    n = row_values.shape[1]
    on_diagonal = lax.broadcasted_iota(jnp.int32, (n, n), 0) == lax.broadcasted_iota(
        jnp.int32, (n, n), 1
    )
    return jnp.sum(jnp.where(on_diagonal, row_values, 0.0), axis=1, keepdims=True)


def probs_kernel(
    tiles, half_slots, cell_hbm, power_hbm, tile_hbm, shadow_hbm, out_ref, cell_ref, power_ref, tile_ref, shadow_ref, sems
):
    sites = shadow_ref.shape[0]
    receivers = out_ref.shape[0]
    strips = shadow_ref.shape[1] // receivers // LANES
    pieces = sems.shape[0] - 3
    span = shadow_ref.shape[1] // pieces
    small = [
        pltpu.make_async_copy(source, target, sems.at[pieces + i])
        for i, (source, target) in enumerate(
            [(cell_hbm, cell_ref), (power_hbm, power_ref), (tile_hbm, tile_ref)]
        )
    ]
    windows = []
    for i in range(pieces):
        part = slice(i * span, (i + 1) * span)
        windows.append(
            pltpu.make_async_copy(shadow_hbm.at[:, part], shadow_ref.at[:, part], sems.at[i])
        )
    for copy in small + windows:
        copy.start()
    for copy in small:
        copy.wait()
    tile_row = tile_ref[...].astype(jnp.float32)
    before = lax.broadcasted_iota(jnp.int32, (sites, sites), 0) < lax.broadcasted_iota(
        jnp.int32, (sites, sites), 1
    )
    same = column(tile_row) == tile_row
    rank = jnp.sum(jnp.where(same & before, 1.0, 0.0), axis=0, keepdims=True)
    core = tile_row - 2.0 * jnp.floor(tile_row * 0.5)
    chip = (tile_row - core) * 0.5
    slot = core * half_slots + rank * (tiles // 2) + chip
    slot_rows = jnp.broadcast_to(
        jnp.concatenate([slot] * (LANES // sites), axis=1), (8, LANES)
    ).astype(jnp.bfloat16)

    lane = lax.broadcasted_iota(jnp.int32, (sites, LANES), 1)
    cell = cell_ref[...].astype(jnp.float32)
    row_gap = (lane // WIN).astype(jnp.float32) - column(cell[0:1, :])
    col_gap = (lane % WIN).astype(jnp.float32) - column(cell[1:2, :])
    col_part = 1.0 + col_gap * col_gap / reach_sq
    row_quarter = row_gap * 0.25
    power = jnp.broadcast_to(column(power_ref[...]), (sites, LANES))

    for block in range(receivers):
        out_ref[block, strips * sites : strips * sites + 8, :] = slot_rows
        for strip in range(strips):
            first = (block * strips + strip) * LANES
            if first % span == 0:
                windows[first // span].wait()
            window = shadow_ref[:, first : first + LANES].astype(jnp.float32)
            row_part = row_quarter + (first // WIN) * 0.25
            loss = col_part + row_part * row_part
            odds_against = loss * jnp.exp(-(power + window))
            out_ref[block, strip * sites : (strip + 1) * sites, :] = (
                1.0 / (1.0 + odds_against)
            ).astype(jnp.bfloat16)


def join_pair(states, hit_a, hit_b):
    miss_a = 1.0 - hit_a
    miss_b = 1.0 - hit_b
    none = miss_a * miss_b
    both = hit_a * hit_b
    one = (hit_a + hit_b) - (both + both)
    new = []
    for k in range(KMAX):
        term = states[k] * none
        if k >= 1:
            term = term + states[k - 1] * one
        if k >= 2:
            term = term + states[k - 2] * both
        new.append(term)
    return new


def count_kernel(for_partner, rows, capacity, sites, blocks_ref, out_ref, *slots_refs):
    senders = blocks_ref.shape[0]
    width = slots_refs[0].shape[1]
    strips = width // LANES
    slots = rows * capacity
    core = lax.axis_index("core")
    half = 1 - core if for_partner else core
    first_slot = (half * slots).astype(jnp.float32)
    slot_number = lax.broadcasted_iota(jnp.int32, (slots, sites), 0).astype(jnp.float32) + first_slot

    def place(sender, slots_ref):
        named = blocks_ref[sender, strips * sites : strips * sites + 8, :].astype(jnp.float32)
        selector = (slot_number == named[0:1, :sites]).astype(jnp.bfloat16)
        probs = jnp.concatenate(
            [blocks_ref[sender, i * sites : (i + 1) * sites, :] for i in range(strips)], axis=1
        )
        slots_ref[...] = jnp.dot(selector, probs, preferred_element_type=jnp.float32)

    states = [jnp.ones((rows, width), jnp.float32)] + [
        jnp.zeros((rows, width), jnp.float32) for _ in range(KMAX - 1)
    ]
    ahead = len(slots_refs)
    for sender in range(min(ahead, senders)):
        place(sender, slots_refs[sender])
    for sender in range(senders):
        slots_ref = slots_refs[sender % ahead]
        for rank in range(0, capacity, 2):
            states = join_pair(
                states,
                slots_ref[rank * rows : (rank + 1) * rows, :],
                slots_ref[(rank + 1) * rows : (rank + 2) * rows, :],
            )
        if sender + ahead < senders:
            place(sender + ahead, slots_ref)
    for k in range(KMAX):
        for strip in range(strips):
            first = (strip * KMAX + k) * rows
            out_ref[first : first + rows, :] = states[k][:, strip * LANES : (strip + 1) * LANES]


def join_kernel(rows, own_ref, got_ref, out_ref):
    strips = own_ref.shape[0] // (KMAX * rows)
    for strip in range(strips):
        parts = []
        for ref in (own_ref, got_ref):
            firsts = [(strip * KMAX + k) * rows for k in range(KMAX)]
            parts.append([ref[first : first + rows, :] for first in firsts])
        own, got = parts
        for k in range(KMAX):
            term = own[0] * got[k]
            for i in range(1, k + 1):
                term = term + own[i] * got[k - i]
            out_ref[pl.ds(strip * KMAX + k, rows, stride=strips * KMAX), :] = term


def merge_kernel(parts, in_ref, out_ref):
    pieces = in_ref.shape[0] // parts
    strips = in_ref.shape[1] // KMAX
    count = lax.broadcasted_iota(jnp.int32, (KMAX, LANES), 0)
    for piece in range(pieces):
        for strip in range(strips):
            rows = slice(strip * KMAX, (strip + 1) * KMAX)
            total = in_ref[piece, rows, :]
            for part in range(1, parts):
                other = in_ref[part * pieces + piece, rows, :]
                joint = other * total[0:1, :]
                for k in range(1, KMAX):
                    shifted = jnp.where(count >= k, pltpu.roll(other, k, 0), 0.0)
                    joint = joint + shifted * total[k : k + 1, :]
                total = joint
            first = (piece * strips + strip) * LANES
            out_ref[0, :, first : first + LANES] = total


def on_device(site_cell, site_power, site_tile, shadow):
    groups = lax.axis_size("grp")
    parts = lax.axis_size("far")
    near = lax.axis_size("near")
    cores = lax.axis_size("core")
    chips = parts * near
    tiles = chips * cores
    sites, cells = shadow.shape
    capacity = max(2, 2 * sites // tiles)
    receivers = groups * near
    width = cells // receivers
    rows = sites * (width // LANES) + 8
    small = pltpu.CompilerParams(vmem_limit_bytes=8 * 1024 * 1024)

    blocks = pl.pallas_call(
        functools.partial(probs_kernel, tiles, chips * capacity),
        out_shape=jax.ShapeDtypeStruct((receivers, rows, LANES), jnp.bfloat16),
        in_specs=[pl.BlockSpec(memory_space=pltpu.HBM)] * 4,
        scratch_shapes=[
            pltpu.VMEM((2, sites), jnp.int32),
            pltpu.VMEM((1, sites), jnp.float32),
            pltpu.VMEM((1, sites), jnp.int32),
            pltpu.VMEM((sites, cells), jnp.bfloat16),
            pltpu.SemaphoreType.DMA((4 + 3,)),
        ],
        compiler_params=small,
        name="probs",
    )(
        *[
            pltpu.with_memory_space_constraint(x, pltpu.HBM)
            for x in (site_cell.T, site_power[None, :], site_tile.T, shadow)
        ]
    )
    blocks = lax.all_to_all(blocks, ("grp", "near"), split_axis=0, concat_axis=0, tiled=True)

    dist_shape = (chips * KMAX * width // LANES, LANES)
    work = chips * width * receivers * capacity * 23

    def counts(for_partner):
        return pl.pallas_call(
            functools.partial(count_kernel, for_partner, chips, capacity, sites),
            out_shape=jax.ShapeDtypeStruct(dist_shape, jnp.float32),
            scratch_shapes=[pltpu.VMEM((chips * capacity, width), jnp.float32)] * 2,
            compiler_params=small,
            cost_estimate=pl.CostEstimate(flops=work, bytes_accessed=4 * work // 23, transcendentals=0),
            name="counts_partner" if for_partner else "counts_own",
        )(blocks)

    swap = [(i, i ^ 1) for i in range(cores)]
    got = lax.ppermute(counts(True), "core", swap)
    dist = pl.pallas_call(
        functools.partial(join_kernel, chips),
        out_shape=jax.ShapeDtypeStruct(dist_shape, jnp.float32),
        compiler_params=small,
        name="join",
    )(counts(False), got)
    dist = dist.reshape(chips, KMAX * width // LANES, LANES)
    dist = lax.all_to_all(dist, ("far", "near"), split_axis=0, concat_axis=0, tiled=True)
    return pl.pallas_call(
        functools.partial(merge_kernel, parts),
        out_shape=jax.ShapeDtypeStruct((1, KMAX, cells // groups), jnp.float32),
        compiler_params=small,
        name="merge",
    )(dist)


def solution(mesh):
    groups, tiles = mesh.shape["grp"], mesh.shape["tile"]
    near = max(1, min(tiles // 4, WIN * WIN // LANES // groups))
    names = ("grp", "far", "near", "core")
    split = Mesh(mesh.devices.reshape(groups, tiles // (2 * near), near, 2), names)
    placed = (P(names, None), P(names), P(names, None), P(names, None))
    return jax.shard_map(
        on_device,
        mesh=split,
        in_specs=placed,
        out_specs=P(("far", "near", "core"), None, "grp"),
        check_vma=False,
    )
```

```python
import functools

import jax
import jax.numpy as jnp
from jax import lax
from jax.experimental import pallas as pl
from jax.experimental.pallas import tpu as pltpu
from jax.sharding import Mesh, PartitionSpec as P

WIN = 64
KMAX = 8
LANES = 128

reach_sq = 16.0
LOG2E = 1.4426950408889634


def column(row_values):
    n = row_values.shape[1]
    on_diagonal = lax.broadcasted_iota(jnp.int32, (n, n), 0) == lax.broadcasted_iota(
        jnp.int32, (n, n), 1
    )
    return jnp.sum(jnp.where(on_diagonal, row_values, 0.0), axis=1, keepdims=True)


def probs_kernel(
    tiles, half_slots, cell_hbm, power_hbm, tile_hbm, shadow_hbm, out_ref, cell_ref, power_ref, tile_ref, shadow_ref, sems
):
    sites = shadow_ref.shape[0]
    receivers = out_ref.shape[0]
    strips = shadow_ref.shape[1] // receivers // LANES
    pieces = sems.shape[0] - 3
    span = shadow_ref.shape[1] // pieces
    small = [
        pltpu.make_async_copy(source, target, sems.at[pieces + i])
        for i, (source, target) in enumerate(
            [(cell_hbm, cell_ref), (power_hbm, power_ref), (tile_hbm, tile_ref)]
        )
    ]
    windows = []
    for i in range(pieces):
        part = slice(i * span, (i + 1) * span)
        windows.append(
            pltpu.make_async_copy(shadow_hbm.at[:, part], shadow_ref.at[:, part], sems.at[i])
        )
    for copy in small + windows:
        copy.start()
    for copy in small:
        copy.wait()
    tile_row = tile_ref[...].astype(jnp.float32)
    before = lax.broadcasted_iota(jnp.int32, (sites, sites), 0) < lax.broadcasted_iota(
        jnp.int32, (sites, sites), 1
    )
    same = column(tile_row) == tile_row
    rank = jnp.sum(jnp.where(same & before, 1.0, 0.0), axis=0, keepdims=True)
    core = tile_row - 2.0 * jnp.floor(tile_row * 0.5)
    chip = (tile_row - core) * 0.5
    slot = core * half_slots + rank * (tiles // 2) + chip
    slot_rows = jnp.broadcast_to(
        jnp.concatenate([slot] * (LANES // sites), axis=1), (8, LANES)
    ).astype(jnp.bfloat16)

    lane = lax.broadcasted_iota(jnp.int32, (sites, LANES), 1)
    cell = cell_ref[...].astype(jnp.float32)
    row_gap = (lane // WIN).astype(jnp.float32) - column(cell[0:1, :])
    col_gap = (lane % WIN).astype(jnp.float32) - column(cell[1:2, :])
    loss = 1.0 + (row_gap * row_gap + col_gap * col_gap) * (1.0 / reach_sq)
    rise = LANES // WIN
    step = (2.0 * rise * row_gap + rise * rise) * (1.0 / reach_sq)
    step_rise = 2.0 * rise * rise / reach_sq
    power = jnp.broadcast_to(column(power_ref[...]) * -LOG2E, (sites, LANES))

    for block in range(receivers):
        out_ref[block, strips * sites : strips * sites + 8, :] = slot_rows
        for strip in range(strips):
            first = (block * strips + strip) * LANES
            if first % span == 0:
                windows[first // span].wait()
            window = shadow_ref[:, first : first + LANES].astype(jnp.float32)
            odds_against = loss * jnp.exp2(power - window * LOG2E)
            out_ref[block, strip * sites : (strip + 1) * sites, :] = (
                1.0 / (1.0 + odds_against)
            ).astype(jnp.bfloat16)
            loss = loss + step
            step = step + step_rise


def join_pair(states, hit_a, hit_b):
    miss_a = 1.0 - hit_a
    miss_b = 1.0 - hit_b
    none = miss_a * miss_b
    both = hit_a * hit_b
    one = (hit_a + hit_b) - (both + both)
    if states is None:
        return [none, one, both]
    new = []
    for k in range(min(len(states) + 2, KMAX)):
        terms = [
            states[k - i] * factor
            for i, factor in enumerate((none, one, both))
            if 0 <= k - i < len(states)
        ]
        new.append(functools.reduce(jnp.add, terms))
    return new


def count_sites(states, half, senders, capacity, sites, blocks_ref, slots_refs):
    slots, width = slots_refs[0].shape
    rows = slots // capacity
    strips = width // LANES
    first_slot = jnp.asarray(half * slots).astype(jnp.float32)
    slot_number = lax.broadcasted_iota(jnp.int32, (slots, sites), 0).astype(jnp.float32) + first_slot

    def place(sender, slots_ref):
        named = blocks_ref[sender, strips * sites : strips * sites + 8, :].astype(jnp.float32)
        selector = (slot_number == named[0:1, :sites]).astype(jnp.bfloat16)
        probs = jnp.concatenate(
            [blocks_ref[sender, i * sites : (i + 1) * sites, :] for i in range(strips)], axis=1
        )
        slots_ref[...] = jnp.dot(selector, probs, preferred_element_type=jnp.float32)

    ahead = min(len(slots_refs), senders)
    for sender in range(ahead):
        place(sender, slots_refs[sender])
    for sender in range(senders):
        slots_ref = slots_refs[sender % ahead]
        for rank in range(0, capacity, 2):
            states = join_pair(
                states,
                slots_ref[rank * rows : (rank + 1) * rows, :],
                slots_ref[(rank + 1) * rows : (rank + 2) * rows, :],
            )
        if sender + ahead < senders:
            place(sender + ahead, slots_ref)
    return states


def keep_states(states, dist_ref):
    rows, width = states[0].shape
    for k in range(KMAX):
        for strip in range(width // LANES):
            first = (strip * KMAX + k) * rows
            dist_ref[first : first + rows, :] = (
                states[k][:, strip * LANES : (strip + 1) * LANES]
                if k < len(states)
                else jnp.zeros((rows, LANES), jnp.float32)
            )


def strip_states(dist_ref, rows, strip):
    firsts = [(strip * KMAX + k) * rows for k in range(KMAX)]
    return [dist_ref[first : first + rows, :] for first in firsts]


def count_kernel(for_partner, capacity, sites, blocks_ref, out_ref, *slots_refs):
    core = lax.axis_index("core")
    half = 1 - core if for_partner else core
    senders = blocks_ref.shape[0]
    keep_states(count_sites(None, half, senders, capacity, sites, blocks_ref, slots_refs), out_ref)


def join_kernel(rows, own_ref, got_ref, out_ref):
    strips = own_ref.shape[0] // (KMAX * rows)
    for strip in range(strips):
        own = strip_states(own_ref, rows, strip)
        got = strip_states(got_ref, rows, strip)
        for k in range(KMAX):
            term = own[0] * got[k]
            for i in range(1, k + 1):
                term = term + own[i] * got[k - i]
            out_ref[pl.ds(strip * KMAX + k, rows, stride=strips * KMAX), :] = term


def merge_kernel(parts, in_ref, out_ref):
    pieces = in_ref.shape[0] // parts
    strips = in_ref.shape[1] // KMAX
    count = lax.broadcasted_iota(jnp.int32, (KMAX, LANES), 0)
    for piece in range(pieces):
        for strip in range(strips):
            rows = slice(strip * KMAX, (strip + 1) * KMAX)
            total = in_ref[piece, rows, :]
            for part in range(1, parts):
                other = in_ref[part * pieces + piece, rows, :]
                joint = other * total[0:1, :]
                for k in range(1, KMAX):
                    shifted = jnp.where(count >= k, pltpu.roll(other, k, 0), 0.0)
                    joint = joint + shifted * total[k : k + 1, :]
                total = joint
            first = (piece * strips + strip) * LANES
            out_ref[0, :, first : first + LANES] = total


def on_device(site_cell, site_power, site_tile, shadow):
    groups = lax.axis_size("grp")
    parts = lax.axis_size("far")
    near = lax.axis_size("near")
    chips = parts * near
    tiles = chips * lax.axis_size("core")
    sites, cells = shadow.shape
    capacity = max(2, 2 * sites // tiles)
    receivers = groups * near
    width = cells // receivers
    rows = sites * (width // LANES) + 8
    small = pltpu.CompilerParams(vmem_limit_bytes=8 * 1024 * 1024)

    blocks = pl.pallas_call(
        functools.partial(probs_kernel, tiles, chips * capacity),
        out_shape=jax.ShapeDtypeStruct((receivers, rows, LANES), jnp.bfloat16),
        in_specs=[pl.BlockSpec(memory_space=pltpu.HBM)] * 4,
        scratch_shapes=[
            pltpu.VMEM((2, sites), jnp.int32),
            pltpu.VMEM((1, sites), jnp.float32),
            pltpu.VMEM((1, sites), jnp.int32),
            pltpu.VMEM((sites, cells), jnp.bfloat16),
            pltpu.SemaphoreType.DMA((4 + 3,)),
        ],
        compiler_params=small,
        name="probs",
    )(
        *[
            pltpu.with_memory_space_constraint(x, pltpu.HBM)
            for x in (site_cell.T, site_power[None, :], site_tile.T, shadow)
        ]
    )
    blocks = lax.all_to_all(blocks, ("grp", "near"), split_axis=0, concat_axis=0, tiled=True)

    dist_shape = (chips * KMAX * width // LANES, LANES)
    work = chips * width * receivers * capacity * 23

    def counts(for_partner):
        return pl.pallas_call(
            functools.partial(count_kernel, for_partner, capacity, sites),
            out_shape=jax.ShapeDtypeStruct(dist_shape, jnp.float32),
            scratch_shapes=[pltpu.VMEM((chips * capacity, width), jnp.float32)] * 2,
            compiler_params=small,
            cost_estimate=pl.CostEstimate(flops=work, bytes_accessed=4 * work // 23, transcendentals=0),
            name="counts_partner" if for_partner else "counts_own",
        )(blocks)

    swap = [(i, i ^ 1) for i in range(2)]
    got = lax.ppermute(counts(True), "core", swap)
    dist = pl.pallas_call(
        functools.partial(join_kernel, chips),
        out_shape=jax.ShapeDtypeStruct(dist_shape, jnp.float32),
        compiler_params=small,
        name="join",
    )(counts(False), got)
    dist = dist.reshape(chips, KMAX * width // LANES, LANES)
    dist = lax.all_to_all(dist, ("far", "near"), split_axis=0, concat_axis=0, tiled=True)
    return pl.pallas_call(
        functools.partial(merge_kernel, parts),
        out_shape=jax.ShapeDtypeStruct((1, KMAX, cells // groups), jnp.float32),
        compiler_params=small,
        name="merge",
    )(dist)


def solution(mesh):
    groups, tiles = mesh.shape["grp"], mesh.shape["tile"]
    near = max(1, min(tiles // 4, WIN * WIN // LANES // groups))
    names = ("grp", "far", "near", "core")
    split = Mesh(mesh.devices.reshape(groups, tiles // (2 * near), near, 2), names)
    placed = (P(names, None), P(names), P(names, None), P(names, None))
    return jax.shard_map(
        on_device,
        mesh=split,
        in_specs=placed,
        out_specs=P(("far", "near", "core"), None, "grp"),
        check_vma=False,
    )
```

```python
import functools

import jax
import jax.numpy as jnp
from jax import lax
from jax.experimental import pallas as pl
from jax.experimental.pallas import tpu as pltpu
from jax.sharding import Mesh, PartitionSpec as P

WIN = 64
KMAX = 8
LANES = 128

reach_sq = 16.0
LOG2E = 1.4426950408889634


def swapped_chips(chips):
    return chips // 2


def backwards(count):
    return list(range(count))[::-1]


def gray_backwards(count):
    return [i ^ (i >> 1) for i in range(count)][::-1]


gather_order = backwards
exchange_order = gray_backwards


def places(order):
    return [order.index(member) for member in range(len(order))]


def column(row_values):
    n = row_values.shape[1]
    on_diagonal = lax.broadcasted_iota(jnp.int32, (n, n), 0) == lax.broadcasted_iota(
        jnp.int32, (n, n), 1
    )
    return jnp.sum(jnp.where(on_diagonal, row_values, 0.0), axis=1, keepdims=True)


def probs_kernel(
    tiles, half_slots, cell_hbm, power_hbm, tile_hbm, shadow_hbm, out_ref, cell_ref, power_ref, tile_ref, shadow_ref, sems
):
    sites = shadow_ref.shape[0]
    receivers = out_ref.shape[0]
    strips = shadow_ref.shape[1] // receivers // LANES
    pieces = sems.shape[0] - 3
    span = shadow_ref.shape[1] // pieces
    small = [
        pltpu.make_async_copy(source, target, sems.at[pieces + i])
        for i, (source, target) in enumerate(
            [(cell_hbm, cell_ref), (power_hbm, power_ref), (tile_hbm, tile_ref)]
        )
    ]
    windows = []
    for i in range(pieces):
        part = slice(i * span, (i + 1) * span)
        windows.append(
            pltpu.make_async_copy(shadow_hbm.at[:, part], shadow_ref.at[:, part], sems.at[i])
        )
    for copy in small + windows:
        copy.start()
    for copy in small:
        copy.wait()
    tile_row = tile_ref[...].astype(jnp.float32)
    before = lax.broadcasted_iota(jnp.int32, (sites, sites), 0) < lax.broadcasted_iota(
        jnp.int32, (sites, sites), 1
    )
    same = column(tile_row) == tile_row
    rank = jnp.sum(jnp.where(same & before, 1.0, 0.0), axis=0, keepdims=True)
    core = tile_row - 2.0 * jnp.floor(tile_row * 0.5)
    chip = (tile_row - core) * 0.5
    swapped = jnp.where(chip < swapped_chips(tiles // 2), 1.0, 0.0)
    half = core + swapped - 2.0 * core * swapped
    place = jnp.zeros_like(chip)
    for number, where in enumerate(places(exchange_order(tiles // 2))):
        place = jnp.where(chip == number, float(where), place)
    slot = half * half_slots + rank * (tiles // 2) + place
    slot_rows = jnp.broadcast_to(
        jnp.concatenate([slot] * (LANES // sites), axis=1), (8, LANES)
    ).astype(jnp.bfloat16)

    lane = lax.broadcasted_iota(jnp.int32, (sites, LANES), 1)
    cell = cell_ref[...].astype(jnp.float32)
    row_gap = (lane // WIN).astype(jnp.float32) - column(cell[0:1, :])
    col_gap = (lane % WIN).astype(jnp.float32) - column(cell[1:2, :])
    loss = 1.0 + (row_gap * row_gap + col_gap * col_gap) * (1.0 / reach_sq)
    rise = LANES // WIN
    step = (2.0 * rise * row_gap + rise * rise) * (1.0 / reach_sq)
    step_rise = 2.0 * rise * rise / reach_sq
    power = jnp.broadcast_to(column(power_ref[...]) * -LOG2E, (sites, LANES))

    for chunk, block in enumerate(places(gather_order(receivers))):
        out_ref[block, strips * sites : strips * sites + 8, :] = slot_rows
        for strip in range(strips):
            first = (chunk * strips + strip) * LANES
            if first % span == 0:
                windows[first // span].wait()
            window = shadow_ref[:, first : first + LANES].astype(jnp.float32)
            odds_against = loss * jnp.exp2(power - window * LOG2E)
            out_ref[block, strip * sites : (strip + 1) * sites, :] = (
                1.0 / (1.0 + odds_against)
            ).astype(jnp.bfloat16)
            loss = loss + step
            step = step + step_rise


def join_pair(states, hit_a, hit_b):
    miss_a = 1.0 - hit_a
    miss_b = 1.0 - hit_b
    none = miss_a * miss_b
    both = hit_a * hit_b
    one = (hit_a + hit_b) - (both + both)
    if states is None:
        return [none, one, both]
    new = []
    for k in range(min(len(states) + 2, KMAX)):
        terms = [
            states[k - i] * factor
            for i, factor in enumerate((none, one, both))
            if 0 <= k - i < len(states)
        ]
        new.append(functools.reduce(jnp.add, terms))
    return new


def count_sites(states, half, senders, capacity, sites, blocks_ref, slots_refs):
    slots, width = slots_refs[0].shape
    rows = slots // capacity
    strips = width // LANES
    first_slot = jnp.asarray(half * slots).astype(jnp.float32)
    slot_number = lax.broadcasted_iota(jnp.int32, (slots, sites), 0).astype(jnp.float32) + first_slot

    def place(sender, slots_ref):
        named = blocks_ref[sender, strips * sites : strips * sites + 8, :].astype(jnp.float32)
        selector = (slot_number == named[0:1, :sites]).astype(jnp.bfloat16)
        probs = jnp.concatenate(
            [blocks_ref[sender, i * sites : (i + 1) * sites, :] for i in range(strips)], axis=1
        )
        slots_ref[...] = jnp.dot(selector, probs, preferred_element_type=jnp.float32)

    ahead = min(len(slots_refs), senders)
    for sender in range(ahead):
        place(sender, slots_refs[sender])
    for sender in range(senders):
        slots_ref = slots_refs[sender % ahead]
        for rank in range(0, capacity, 2):
            states = join_pair(
                states,
                slots_ref[rank * rows : (rank + 1) * rows, :],
                slots_ref[(rank + 1) * rows : (rank + 2) * rows, :],
            )
        if sender + ahead < senders:
            place(sender + ahead, slots_ref)
    return states


def keep_states(states, dist_ref):
    rows, width = states[0].shape
    for k in range(KMAX):
        for strip in range(width // LANES):
            first = (strip * KMAX + k) * rows
            dist_ref[first : first + rows, :] = (
                states[k][:, strip * LANES : (strip + 1) * LANES]
                if k < len(states)
                else jnp.zeros((rows, LANES), jnp.float32)
            )


def strip_states(dist_ref, rows, strip):
    firsts = [(strip * KMAX + k) * rows for k in range(KMAX)]
    return [dist_ref[first : first + rows, :] for first in firsts]


def count_kernel(for_partner, capacity, sites, blocks_ref, out_ref, *slots_refs):
    rows = slots_refs[0].shape[0] // capacity
    chip = lax.axis_index("far") * lax.axis_size("near") + lax.axis_index("near")
    swapped = jnp.where(chip < swapped_chips(rows), 1, 0)
    half = (lax.axis_index("core") + swapped + (1 if for_partner else 0)) % 2
    senders = blocks_ref.shape[0]
    keep_states(count_sites(None, half, senders, capacity, sites, blocks_ref, slots_refs), out_ref)


def join_kernel(rows, own_ref, got_ref, out_ref):
    strips = own_ref.shape[0] // (KMAX * rows)
    for strip in range(strips):
        own = strip_states(own_ref, rows, strip)
        got = strip_states(got_ref, rows, strip)
        for k in range(KMAX):
            term = own[0] * got[k]
            for i in range(1, k + 1):
                term = term + own[i] * got[k - i]
            out_ref[pl.ds(strip * KMAX + k, rows, stride=strips * KMAX), :] = term


def merge_kernel(parts, in_ref, out_ref):
    pieces = in_ref.shape[0] // parts
    place = places(exchange_order(in_ref.shape[0]))
    strips = in_ref.shape[1] // KMAX
    count = lax.broadcasted_iota(jnp.int32, (KMAX, LANES), 0)
    for piece in range(pieces):
        for strip in range(strips):
            rows = slice(strip * KMAX, (strip + 1) * KMAX)
            total = in_ref[place[piece], rows, :]
            for part in range(1, parts):
                other = in_ref[place[part * pieces + piece], rows, :]
                joint = other * total[0:1, :]
                for k in range(1, KMAX):
                    shifted = jnp.where(count >= k, pltpu.roll(other, k, 0), 0.0)
                    joint = joint + shifted * total[k : k + 1, :]
                total = joint
            first = (piece * strips + strip) * LANES
            out_ref[0, :, first : first + LANES] = total


def on_device(site_cell, site_power, site_tile, shadow):
    groups = lax.axis_size("grp")
    parts = lax.axis_size("far")
    near = lax.axis_size("near")
    chips = parts * near
    tiles = chips * lax.axis_size("core")
    sites, cells = shadow.shape
    capacity = max(2, 2 * sites // tiles)
    receivers = groups * near
    width = cells // receivers
    rows = sites * (width // LANES) + 8
    small = pltpu.CompilerParams(vmem_limit_bytes=8 * 1024 * 1024)

    blocks = pl.pallas_call(
        functools.partial(probs_kernel, tiles, chips * capacity),
        out_shape=jax.ShapeDtypeStruct((receivers, rows, LANES), jnp.bfloat16),
        in_specs=[pl.BlockSpec(memory_space=pltpu.HBM)] * 4,
        scratch_shapes=[
            pltpu.VMEM((2, sites), jnp.int32),
            pltpu.VMEM((1, sites), jnp.float32),
            pltpu.VMEM((1, sites), jnp.int32),
            pltpu.VMEM((sites, cells), jnp.bfloat16),
            pltpu.SemaphoreType.DMA((4 + 3,)),
        ],
        compiler_params=small,
        name="probs",
    )(
        *[
            pltpu.with_memory_space_constraint(x, pltpu.HBM)
            for x in (site_cell.T, site_power[None, :], site_tile.T, shadow)
        ]
    )
    gather = [
        [
            ((member // near * parts + far) * near + member % near) * 2 + half
            for member in gather_order(receivers)
        ]
        for far in range(parts)
        for half in (0, 1)
    ]
    blocks = lax.all_to_all(
        blocks,
        ("grp", "far", "near", "core"),
        split_axis=0,
        concat_axis=0,
        axis_index_groups=gather,
        tiled=True,
    )

    dist_shape = (chips * KMAX * width // LANES, LANES)
    work = chips * width * receivers * capacity * 23

    def counts(for_partner):
        return pl.pallas_call(
            functools.partial(count_kernel, for_partner, capacity, sites),
            out_shape=jax.ShapeDtypeStruct(dist_shape, jnp.float32),
            scratch_shapes=[pltpu.VMEM((chips * capacity, width), jnp.float32)] * 2,
            compiler_params=small,
            cost_estimate=pl.CostEstimate(flops=work, bytes_accessed=4 * work // 23, transcendentals=0),
            name="counts_partner" if for_partner else "counts_own",
        )(blocks)

    swap = [(i, i ^ 1) for i in range(2)]
    got = lax.ppermute(counts(True), "core", swap)
    dist = pl.pallas_call(
        functools.partial(join_kernel, chips),
        out_shape=jax.ShapeDtypeStruct(dist_shape, jnp.float32),
        compiler_params=small,
        name="join",
    )(counts(False), got)
    dist = dist.reshape(chips, KMAX * width // LANES, LANES)
    exchange = [
        [2 * chip + (half ^ (1 if chip < swapped_chips(chips) else 0)) for chip in exchange_order(chips)]
        for half in (0, 1)
    ]
    dist = lax.all_to_all(
        dist,
        ("far", "near", "core"),
        split_axis=0,
        concat_axis=0,
        axis_index_groups=exchange,
        tiled=True,
    )
    return pl.pallas_call(
        functools.partial(merge_kernel, parts),
        out_shape=jax.ShapeDtypeStruct((1, KMAX, cells // groups), jnp.float32),
        compiler_params=small,
        name="merge",
    )(dist)


def solution(mesh):
    groups, tiles = mesh.shape["grp"], mesh.shape["tile"]
    near = max(1, min(tiles // 4, WIN * WIN // LANES // groups))
    names = ("grp", "far", "near", "core")
    split = Mesh(mesh.devices.reshape(groups, tiles // (2 * near), near, 2), names)
    placed = (P(names, None), P(names), P(names, None), P(names, None))
    return jax.shard_map(
        on_device,
        mesh=split,
        in_specs=placed,
        out_specs=P(("far", "near", "core"), None, "grp"),
        check_vma=False,
    )
```

```python
import functools

import jax
import jax.numpy as jnp
from jax import lax
from jax.experimental import pallas as pl
from jax.experimental.pallas import tpu as pltpu
from jax.sharding import Mesh, PartitionSpec as P

WIN = 64
KMAX = 8
LANES = 128

reach_sq = 16.0
LOG2E = 1.4426950408889634


def swapped_chips(chips):
    return chips // 2


GATHER_ORDER = (6, 7, 2, 4, 0, 3, 1, 5)
EXCHANGE_ORDER = (4, 2, 5, 1, 0, 7, 3, 6)


def gather_order(count):
    return list(GATHER_ORDER) if count == len(GATHER_ORDER) else list(range(count))[::-1]


def exchange_order(count):
    return list(EXCHANGE_ORDER) if count == len(EXCHANGE_ORDER) else list(range(count))[::-1]


def places(order):
    return [order.index(member) for member in range(len(order))]


def column(row_values):
    n = row_values.shape[1]
    on_diagonal = lax.broadcasted_iota(jnp.int32, (n, n), 0) == lax.broadcasted_iota(
        jnp.int32, (n, n), 1
    )
    return jnp.sum(jnp.where(on_diagonal, row_values, 0.0), axis=1, keepdims=True)


def probs_kernel(
    tiles, half_slots, cell_hbm, power_hbm, tile_hbm, shadow_hbm, out_ref, cell_ref, power_ref, tile_ref, shadow_ref, sems
):
    sites = shadow_ref.shape[0]
    receivers = out_ref.shape[0]
    strips = shadow_ref.shape[1] // receivers // LANES
    pieces = sems.shape[0] - 3
    span = shadow_ref.shape[1] // pieces
    small = [
        pltpu.make_async_copy(source, target, sems.at[pieces + i])
        for i, (source, target) in enumerate(
            [(cell_hbm, cell_ref), (power_hbm, power_ref), (tile_hbm, tile_ref)]
        )
    ]
    windows = []
    for i in range(pieces):
        part = slice(i * span, (i + 1) * span)
        windows.append(
            pltpu.make_async_copy(shadow_hbm.at[:, part], shadow_ref.at[:, part], sems.at[i])
        )
    for copy in small + windows:
        copy.start()
    for copy in small:
        copy.wait()
    tile_row = tile_ref[...].astype(jnp.float32)
    before = lax.broadcasted_iota(jnp.int32, (sites, sites), 0) < lax.broadcasted_iota(
        jnp.int32, (sites, sites), 1
    )
    same = column(tile_row) == tile_row
    rank = jnp.sum(jnp.where(same & before, 1.0, 0.0), axis=0, keepdims=True)
    core = tile_row - 2.0 * jnp.floor(tile_row * 0.5)
    chip = (tile_row - core) * 0.5
    swapped = jnp.where(chip < swapped_chips(tiles // 2), 1.0, 0.0)
    half = core + swapped - 2.0 * core * swapped
    place = jnp.zeros_like(chip)
    for number, where in enumerate(places(exchange_order(tiles // 2))):
        place = jnp.where(chip == number, float(where), place)
    slot = half * half_slots + rank * (tiles // 2) + place
    slot_rows = jnp.broadcast_to(
        jnp.concatenate([slot] * (LANES // sites), axis=1), (8, LANES)
    ).astype(jnp.bfloat16)

    lane = lax.broadcasted_iota(jnp.int32, (sites, LANES), 1)
    cell = cell_ref[...].astype(jnp.float32)
    row_gap = (lane // WIN).astype(jnp.float32) - column(cell[0:1, :])
    col_gap = (lane % WIN).astype(jnp.float32) - column(cell[1:2, :])
    loss = 1.0 + (row_gap * row_gap + col_gap * col_gap) * (1.0 / reach_sq)
    rise = LANES // WIN
    step = (2.0 * rise * row_gap + rise * rise) * (1.0 / reach_sq)
    step_rise = 2.0 * rise * rise / reach_sq
    power = jnp.broadcast_to(column(power_ref[...]) * -LOG2E, (sites, LANES))

    for chunk, block in enumerate(places(gather_order(receivers))):
        out_ref[block, strips * sites : strips * sites + 8, :] = slot_rows
        for strip in range(strips):
            first = (chunk * strips + strip) * LANES
            if first % span == 0:
                windows[first // span].wait()
            window = shadow_ref[:, first : first + LANES].astype(jnp.float32)
            odds_against = loss * jnp.exp2(power - window * LOG2E)
            out_ref[block, strip * sites : (strip + 1) * sites, :] = (
                1.0 / (1.0 + odds_against)
            ).astype(jnp.bfloat16)
            loss = loss + step
            step = step + step_rise


def join_pair(states, hit_a, hit_b):
    miss_a = 1.0 - hit_a
    miss_b = 1.0 - hit_b
    none = miss_a * miss_b
    both = hit_a * hit_b
    one = (hit_a + hit_b) - (both + both)
    if states is None:
        return [none, one, both]
    new = []
    for k in range(min(len(states) + 2, KMAX)):
        terms = [
            states[k - i] * factor
            for i, factor in enumerate((none, one, both))
            if 0 <= k - i < len(states)
        ]
        new.append(functools.reduce(jnp.add, terms))
    return new


def count_sites(states, half, senders, capacity, sites, blocks_ref, slots_refs):
    slots, width = slots_refs[0].shape
    rows = slots // capacity
    strips = width // LANES
    first_slot = jnp.asarray(half * slots).astype(jnp.float32)
    slot_number = lax.broadcasted_iota(jnp.int32, (slots, sites), 0).astype(jnp.float32) + first_slot

    def place(sender, slots_ref):
        named = blocks_ref[sender, strips * sites : strips * sites + 8, :].astype(jnp.float32)
        selector = (slot_number == named[0:1, :sites]).astype(jnp.bfloat16)
        probs = jnp.concatenate(
            [blocks_ref[sender, i * sites : (i + 1) * sites, :] for i in range(strips)], axis=1
        )
        slots_ref[...] = jnp.dot(selector, probs, preferred_element_type=jnp.float32)

    ahead = min(len(slots_refs), senders)
    for sender in range(ahead):
        place(sender, slots_refs[sender])
    for sender in range(senders):
        slots_ref = slots_refs[sender % ahead]
        for rank in range(0, capacity, 2):
            states = join_pair(
                states,
                slots_ref[rank * rows : (rank + 1) * rows, :],
                slots_ref[(rank + 1) * rows : (rank + 2) * rows, :],
            )
        if sender + ahead < senders:
            place(sender + ahead, slots_ref)
    return states


def keep_states(states, dist_ref):
    rows, width = states[0].shape
    for k in range(KMAX):
        for strip in range(width // LANES):
            first = (strip * KMAX + k) * rows
            dist_ref[first : first + rows, :] = (
                states[k][:, strip * LANES : (strip + 1) * LANES]
                if k < len(states)
                else jnp.zeros((rows, LANES), jnp.float32)
            )


def strip_states(dist_ref, rows, strip):
    firsts = [(strip * KMAX + k) * rows for k in range(KMAX)]
    return [dist_ref[first : first + rows, :] for first in firsts]


def count_kernel(for_partner, capacity, sites, blocks_ref, out_ref, *slots_refs):
    rows = slots_refs[0].shape[0] // capacity
    chip = lax.axis_index("far") * lax.axis_size("near") + lax.axis_index("near")
    swapped = jnp.where(chip < swapped_chips(rows), 1, 0)
    half = (lax.axis_index("core") + swapped + (1 if for_partner else 0)) % 2
    senders = blocks_ref.shape[0]
    keep_states(count_sites(None, half, senders, capacity, sites, blocks_ref, slots_refs), out_ref)


def join_kernel(rows, own_ref, got_ref, out_ref):
    strips = own_ref.shape[0] // (KMAX * rows)
    for strip in range(strips):
        own = strip_states(own_ref, rows, strip)
        got = strip_states(got_ref, rows, strip)
        for k in range(KMAX):
            term = own[0] * got[k]
            for i in range(1, k + 1):
                term = term + own[i] * got[k - i]
            out_ref[pl.ds(strip * KMAX + k, rows, stride=strips * KMAX), :] = term


def merge_kernel(parts, in_ref, out_ref):
    pieces = in_ref.shape[0] // parts
    place = places(exchange_order(in_ref.shape[0]))
    strips = in_ref.shape[1] // KMAX
    count = lax.broadcasted_iota(jnp.int32, (KMAX, LANES), 0)
    for piece in range(pieces):
        for strip in range(strips):
            rows = slice(strip * KMAX, (strip + 1) * KMAX)
            total = in_ref[place[piece], rows, :]
            for part in range(1, parts):
                other = in_ref[place[part * pieces + piece], rows, :]
                joint = other * total[0:1, :]
                for k in range(1, KMAX):
                    shifted = jnp.where(count >= k, pltpu.roll(other, k, 0), 0.0)
                    joint = joint + shifted * total[k : k + 1, :]
                total = joint
            first = (piece * strips + strip) * LANES
            out_ref[0, :, first : first + LANES] = total


def on_device(site_cell, site_power, site_tile, shadow):
    groups = lax.axis_size("grp")
    parts = lax.axis_size("far")
    near = lax.axis_size("near")
    chips = parts * near
    tiles = chips * lax.axis_size("core")
    sites, cells = shadow.shape
    capacity = max(2, 2 * sites // tiles)
    receivers = groups * near
    width = cells // receivers
    rows = sites * (width // LANES) + 8
    small = pltpu.CompilerParams(vmem_limit_bytes=8 * 1024 * 1024)

    blocks = pl.pallas_call(
        functools.partial(probs_kernel, tiles, chips * capacity),
        out_shape=jax.ShapeDtypeStruct((receivers, rows, LANES), jnp.bfloat16),
        in_specs=[pl.BlockSpec(memory_space=pltpu.HBM)] * 4,
        scratch_shapes=[
            pltpu.VMEM((2, sites), jnp.int32),
            pltpu.VMEM((1, sites), jnp.float32),
            pltpu.VMEM((1, sites), jnp.int32),
            pltpu.VMEM((sites, cells), jnp.bfloat16),
            pltpu.SemaphoreType.DMA((4 + 3,)),
        ],
        compiler_params=small,
        name="probs",
    )(
        *[
            pltpu.with_memory_space_constraint(x, pltpu.HBM)
            for x in (site_cell.T, site_power[None, :], site_tile.T, shadow)
        ]
    )
    gather = [
        [
            ((member // near * parts + far) * near + member % near) * 2 + half
            for member in gather_order(receivers)
        ]
        for far in range(parts)
        for half in (0, 1)
    ]
    blocks = lax.all_to_all(
        blocks,
        ("grp", "far", "near", "core"),
        split_axis=0,
        concat_axis=0,
        axis_index_groups=gather,
        tiled=True,
    )

    dist_shape = (chips * KMAX * width // LANES, LANES)
    work = chips * width * receivers * capacity * 23

    def counts(for_partner):
        return pl.pallas_call(
            functools.partial(count_kernel, for_partner, capacity, sites),
            out_shape=jax.ShapeDtypeStruct(dist_shape, jnp.float32),
            scratch_shapes=[pltpu.VMEM((chips * capacity, width), jnp.float32)] * 2,
            compiler_params=small,
            cost_estimate=pl.CostEstimate(flops=work, bytes_accessed=4 * work // 23, transcendentals=0),
            name="counts_partner" if for_partner else "counts_own",
        )(blocks)

    swap = [(i, i ^ 1) for i in range(2)]
    got = lax.ppermute(counts(True), "core", swap)
    dist = pl.pallas_call(
        functools.partial(join_kernel, chips),
        out_shape=jax.ShapeDtypeStruct(dist_shape, jnp.float32),
        compiler_params=small,
        name="join",
    )(counts(False), got)
    dist = dist.reshape(chips, KMAX * width // LANES, LANES)
    exchange = [
        [2 * chip + (half ^ (1 if chip < swapped_chips(chips) else 0)) for chip in exchange_order(chips)]
        for half in (0, 1)
    ]
    dist = lax.all_to_all(
        dist,
        ("far", "near", "core"),
        split_axis=0,
        concat_axis=0,
        axis_index_groups=exchange,
        tiled=True,
    )
    return pl.pallas_call(
        functools.partial(merge_kernel, parts),
        out_shape=jax.ShapeDtypeStruct((1, KMAX, cells // groups), jnp.float32),
        compiler_params=small,
        name="merge",
    )(dist)


def solution(mesh):
    groups, tiles = mesh.shape["grp"], mesh.shape["tile"]
    near = max(1, min(tiles // 4, WIN * WIN // LANES // groups))
    names = ("grp", "far", "near", "core")
    split = Mesh(mesh.devices.reshape(groups, tiles // (2 * near), near, 2), names)
    placed = (P(names, None), P(names), P(names, None), P(names, None))
    return jax.shard_map(
        on_device,
        mesh=split,
        in_specs=placed,
        out_specs=P(("far", "near", "core"), None, "grp"),
        check_vma=False,
    )
```

```python
import functools

import jax
import jax.numpy as jnp
from jax import lax
from jax.experimental import pallas as pl
from jax.experimental.pallas import tpu as pltpu
from jax.sharding import Mesh, PartitionSpec as P

WIN = 64
KMAX = 8
LANES = 128

reach_sq = 16.0
LOG2E = 1.4426950408889634


def swapped_chips(chips):
    return chips // 2


GATHER_ORDER = (6, 7, 2, 3, 0, 4, 1, 5)
EXCHANGE_ORDER = (4, 2, 5, 6, 0, 7, 3, 1)


def gather_order(count):
    return list(GATHER_ORDER) if count == len(GATHER_ORDER) else list(range(count))[::-1]


def exchange_order(count):
    return list(EXCHANGE_ORDER) if count == len(EXCHANGE_ORDER) else list(range(count))[::-1]


def places(order):
    return [order.index(member) for member in range(len(order))]


def column(row_values):
    n = row_values.shape[1]
    on_diagonal = lax.broadcasted_iota(jnp.int32, (n, n), 0) == lax.broadcasted_iota(
        jnp.int32, (n, n), 1
    )
    return jnp.sum(jnp.where(on_diagonal, row_values, 0.0), axis=1, keepdims=True)


def probs_kernel(
    tiles, half_slots, cell_hbm, power_hbm, tile_hbm, shadow_hbm, out_ref, cell_ref, power_ref, tile_ref, shadow_ref, sems
):
    sites = shadow_ref.shape[0]
    receivers = out_ref.shape[0]
    strips = shadow_ref.shape[1] // receivers // LANES
    pieces = sems.shape[0] - 3
    span = shadow_ref.shape[1] // pieces
    small = [
        pltpu.make_async_copy(source, target, sems.at[pieces + i])
        for i, (source, target) in enumerate(
            [(cell_hbm, cell_ref), (power_hbm, power_ref), (tile_hbm, tile_ref)]
        )
    ]
    windows = []
    for i in range(pieces):
        part = slice(i * span, (i + 1) * span)
        windows.append(
            pltpu.make_async_copy(shadow_hbm.at[:, part], shadow_ref.at[:, part], sems.at[i])
        )
    for copy in small + windows:
        copy.start()
    for copy in small:
        copy.wait()
    tile_row = tile_ref[...].astype(jnp.float32)
    before = lax.broadcasted_iota(jnp.int32, (sites, sites), 0) < lax.broadcasted_iota(
        jnp.int32, (sites, sites), 1
    )
    same = column(tile_row) == tile_row
    rank = jnp.sum(jnp.where(same & before, 1.0, 0.0), axis=0, keepdims=True)
    core = tile_row - 2.0 * jnp.floor(tile_row * 0.5)
    chip = (tile_row - core) * 0.5
    swapped = jnp.where(chip < swapped_chips(tiles // 2), 1.0, 0.0)
    half = core + swapped - 2.0 * core * swapped
    place = jnp.zeros_like(chip)
    for number, where in enumerate(places(exchange_order(tiles // 2))):
        place = jnp.where(chip == number, float(where), place)
    slot = half * half_slots + rank * (tiles // 2) + place
    slot_rows = jnp.broadcast_to(
        jnp.concatenate([slot] * (LANES // sites), axis=1), (8, LANES)
    ).astype(jnp.bfloat16)

    lane = lax.broadcasted_iota(jnp.int32, (sites, LANES), 1)
    cell = cell_ref[...].astype(jnp.float32)
    row_gap = (lane // WIN).astype(jnp.float32) - column(cell[0:1, :])
    col_gap = (lane % WIN).astype(jnp.float32) - column(cell[1:2, :])
    loss = 1.0 + (row_gap * row_gap + col_gap * col_gap) * (1.0 / reach_sq)
    rise = LANES // WIN
    step = (2.0 * rise * row_gap + rise * rise) * (1.0 / reach_sq)
    step_rise = 2.0 * rise * rise / reach_sq
    power = jnp.broadcast_to(column(power_ref[...]) * -LOG2E, (sites, LANES))

    for chunk, block in enumerate(places(gather_order(receivers))):
        out_ref[block, strips * sites : strips * sites + 8, :] = slot_rows
        for strip in range(strips):
            first = (chunk * strips + strip) * LANES
            if first % span == 0:
                windows[first // span].wait()
            window = shadow_ref[:, first : first + LANES].astype(jnp.float32)
            odds_against = loss * jnp.exp2(power - window * LOG2E)
            out_ref[block, strip * sites : (strip + 1) * sites, :] = (
                1.0 / (1.0 + odds_against)
            ).astype(jnp.bfloat16)
            loss = loss + step
            step = step + step_rise


def join_pair(states, hit_a, hit_b):
    miss_a = 1.0 - hit_a
    miss_b = 1.0 - hit_b
    none = miss_a * miss_b
    both = hit_a * hit_b
    one = (hit_a + hit_b) - (both + both)
    if states is None:
        return [none, one, both]
    new = []
    for k in range(min(len(states) + 2, KMAX)):
        terms = [
            states[k - i] * factor
            for i, factor in enumerate((none, one, both))
            if 0 <= k - i < len(states)
        ]
        new.append(functools.reduce(jnp.add, terms))
    return new


def count_sites(states, half, senders, capacity, sites, blocks_ref, slots_refs):
    slots, width = slots_refs[0].shape
    rows = slots // capacity
    strips = width // LANES
    first_slot = jnp.asarray(half * slots).astype(jnp.float32)
    slot_number = lax.broadcasted_iota(jnp.int32, (slots, sites), 0).astype(jnp.float32) + first_slot

    def place(sender, slots_ref):
        named = blocks_ref[sender, strips * sites : strips * sites + 8, :].astype(jnp.float32)
        selector = (slot_number == named[0:1, :sites]).astype(jnp.bfloat16)
        probs = jnp.concatenate(
            [blocks_ref[sender, i * sites : (i + 1) * sites, :] for i in range(strips)], axis=1
        )
        slots_ref[...] = jnp.dot(selector, probs, preferred_element_type=jnp.float32)

    ahead = min(len(slots_refs), senders)
    for sender in range(ahead):
        place(sender, slots_refs[sender])
    for sender in range(senders):
        slots_ref = slots_refs[sender % ahead]
        for rank in range(0, capacity, 2):
            states = join_pair(
                states,
                slots_ref[rank * rows : (rank + 1) * rows, :],
                slots_ref[(rank + 1) * rows : (rank + 2) * rows, :],
            )
        if sender + ahead < senders:
            place(sender + ahead, slots_ref)
    return states


def keep_states(states, dist_ref):
    rows, width = states[0].shape
    for k in range(KMAX):
        for strip in range(width // LANES):
            first = (strip * KMAX + k) * rows
            dist_ref[first : first + rows, :] = (
                states[k][:, strip * LANES : (strip + 1) * LANES]
                if k < len(states)
                else jnp.zeros((rows, LANES), jnp.float32)
            )


def strip_states(dist_ref, rows, strip):
    firsts = [(strip * KMAX + k) * rows for k in range(KMAX)]
    return [dist_ref[first : first + rows, :] for first in firsts]


def count_kernel(for_partner, capacity, sites, blocks_ref, out_ref, *slots_refs):
    rows = slots_refs[0].shape[0] // capacity
    chip = lax.axis_index("far") * lax.axis_size("near") + lax.axis_index("near")
    swapped = jnp.where(chip < swapped_chips(rows), 1, 0)
    half = (lax.axis_index("core") + swapped + (1 if for_partner else 0)) % 2
    senders = blocks_ref.shape[0]
    keep_states(count_sites(None, half, senders, capacity, sites, blocks_ref, slots_refs), out_ref)


def join_kernel(rows, own_ref, got_ref, out_ref):
    strips = own_ref.shape[0] // (KMAX * rows)
    for strip in range(strips):
        own = strip_states(own_ref, rows, strip)
        got = strip_states(got_ref, rows, strip)
        for k in range(KMAX):
            term = own[0] * got[k]
            for i in range(1, k + 1):
                term = term + own[i] * got[k - i]
            out_ref[pl.ds(strip * KMAX + k, rows, stride=strips * KMAX), :] = term


def merge_kernel(parts, in_ref, out_ref):
    pieces = in_ref.shape[0] // parts
    place = places(exchange_order(in_ref.shape[0]))
    strips = in_ref.shape[1] // KMAX
    count = lax.broadcasted_iota(jnp.int32, (KMAX, LANES), 0)
    for piece in range(pieces):
        for strip in range(strips):
            rows = slice(strip * KMAX, (strip + 1) * KMAX)
            total = in_ref[place[piece], rows, :]
            for part in range(1, parts):
                other = in_ref[place[part * pieces + piece], rows, :]
                joint = other * total[0:1, :]
                for k in range(1, KMAX):
                    shifted = jnp.where(count >= k, pltpu.roll(other, k, 0), 0.0)
                    joint = joint + shifted * total[k : k + 1, :]
                total = joint
            first = (piece * strips + strip) * LANES
            out_ref[0, :, first : first + LANES] = total


def on_device(site_cell, site_power, site_tile, shadow):
    groups = lax.axis_size("grp")
    parts = lax.axis_size("far")
    near = lax.axis_size("near")
    chips = parts * near
    tiles = chips * lax.axis_size("core")
    sites, cells = shadow.shape
    capacity = max(2, 2 * sites // tiles)
    receivers = groups * near
    width = cells // receivers
    rows = sites * (width // LANES) + 8
    small = pltpu.CompilerParams(vmem_limit_bytes=8 * 1024 * 1024)

    blocks = pl.pallas_call(
        functools.partial(probs_kernel, tiles, chips * capacity),
        out_shape=jax.ShapeDtypeStruct((receivers, rows, LANES), jnp.bfloat16),
        in_specs=[pl.BlockSpec(memory_space=pltpu.HBM)] * 4,
        scratch_shapes=[
            pltpu.VMEM((2, sites), jnp.int32),
            pltpu.VMEM((1, sites), jnp.float32),
            pltpu.VMEM((1, sites), jnp.int32),
            pltpu.VMEM((sites, cells), jnp.bfloat16),
            pltpu.SemaphoreType.DMA((4 + 3,)),
        ],
        compiler_params=small,
        name="probs",
    )(
        *[
            pltpu.with_memory_space_constraint(x, pltpu.HBM)
            for x in (site_cell.T, site_power[None, :], site_tile.T, shadow)
        ]
    )
    gather = [
        [
            ((member // near * parts + far) * near + member % near) * 2 + half
            for member in gather_order(receivers)
        ]
        for far in range(parts)
        for half in (0, 1)
    ]
    blocks = lax.all_to_all(
        blocks,
        ("grp", "far", "near", "core"),
        split_axis=0,
        concat_axis=0,
        axis_index_groups=gather,
        tiled=True,
    )

    dist_shape = (chips * KMAX * width // LANES, LANES)
    work = chips * width * receivers * capacity * 23

    def counts(for_partner):
        return pl.pallas_call(
            functools.partial(count_kernel, for_partner, capacity, sites),
            out_shape=jax.ShapeDtypeStruct(dist_shape, jnp.float32),
            scratch_shapes=[pltpu.VMEM((chips * capacity, width), jnp.float32)] * 2,
            compiler_params=small,
            cost_estimate=pl.CostEstimate(flops=work, bytes_accessed=4 * work // 23, transcendentals=0),
            name="counts_partner" if for_partner else "counts_own",
        )(blocks)

    swap = [(i, i ^ 1) for i in range(2)]
    got = lax.ppermute(counts(True), "core", swap)
    dist = pl.pallas_call(
        functools.partial(join_kernel, chips),
        out_shape=jax.ShapeDtypeStruct(dist_shape, jnp.float32),
        compiler_params=small,
        name="join",
    )(counts(False), got)
    dist = dist.reshape(chips, KMAX * width // LANES, LANES)
    exchange = [
        [2 * chip + (half ^ (1 if chip < swapped_chips(chips) else 0)) for chip in exchange_order(chips)]
        for half in (0, 1)
    ]
    dist = lax.all_to_all(
        dist,
        ("far", "near", "core"),
        split_axis=0,
        concat_axis=0,
        axis_index_groups=exchange,
        tiled=True,
    )
    return pl.pallas_call(
        functools.partial(merge_kernel, parts),
        out_shape=jax.ShapeDtypeStruct((1, KMAX, cells // groups), jnp.float32),
        compiler_params=small,
        name="merge",
    )(dist)


def solution(mesh):
    groups, tiles = mesh.shape["grp"], mesh.shape["tile"]
    near = max(1, min(tiles // 4, WIN * WIN // LANES // groups))
    names = ("grp", "far", "near", "core")
    split = Mesh(mesh.devices.reshape(groups, tiles // (2 * near), near, 2), names)
    placed = (P(names, None), P(names), P(names, None), P(names, None))
    return jax.shard_map(
        on_device,
        mesh=split,
        in_specs=placed,
        out_specs=P(("far", "near", "core"), None, "grp"),
        check_vma=False,
    )
```
